32 devices in a mesh: group: 4 (over z), dom: 8 (over y, x, core).
Axes of the slice: x: 2, y: 2, z: 4, core: 2. Of those that a mesh axis runs over, the one named last changes fastest.
Arguments:
- hot_rows: bfloat16 [4096, 1024], P(('group', 'dom')), may hold values from -6 to 6
- cold_codes: bfloat16 [4096, 1024], P(('group', 'dom')), may hold values from -127 to 127
- scale_index: int32 [4096], P(('group', 'dom')), may hold values from 0 to 255
- scale_table: float32 [256], replicated, may hold values from 0.004 to 0.04
- stale_rows: bfloat16 [4096, 1024], P(('group', 'dom')), may hold values from -6 to 6
- tile_index: int32 [64, 3], P(('group', 'dom')), may hold values from 0 to 2
- tile_count: int32 [64], P(('group', 'dom')), may hold values from 1 to 3
- tile_values: bfloat16 [64, 3, 128, 128], P(('group', 'dom')), may hold values from -0.3125 to 0.3125
- weight: bfloat16 [1024, 1024], P('dom'), may hold values from -0.1875 to 0.1875
- out_grad: bfloat16 [8192, 1024], P(('group', 'dom')), may hold values from -6 to 6
- stale_grads: bfloat16 [4096, 1024], P(('group', 'dom')), may hold values from -6 to 6
- send_rows: int32 [256, 16], P(('group', 'dom')), may hold values from 0 to 255
Outputs:
- activations: bfloat16 [8192, 1024], P(('group', 'dom'))
- feature_grad: bfloat16 [8192, 1024], P(('group', 'dom'))
- weight_grad: float32 [1024, 1024], P('dom')
- next_rows: bfloat16 [4096, 1024], P(('group', 'dom'))
- next_grads: bfloat16 [4096, 1024], P(('group', 'dom'))
The draws below stay inside these ranges and needn't reach their ends.
Inputs may be any that keep to these rules, and one draw needn't show every extreme that they name: `send_rows`: rows may repeat.
All inputs are finite; a program needn't handle non-finite values.
Results may differ from the reference program's by a relative error of at most 0.0061.
Values may be sent and summed in bfloat16 or wider, within the bound.
A program may use at most 64 MiB of HBM per device.

```python
import math
import jax
import jax.numpy as jnp
from jax import lax

D = 1024
CLUSTER = 128
HOT_CL = 1
COLD_CL = 1
TILES = 3
BND_ROWS = 128
NSCALE = 256
CL = 2
ROWS = 256
SRC_CL = 3
PEER_ROWS = 16
N_GROUP = 4
N_DOM = 8
DEVICES = 32


def touch_ends(drawn, own_key, smallest, high):
    spot = [jax.random.randint(jax.random.fold_in(own_key, axis), (), 0, length) for axis, length in enumerate(drawn.shape)]
    longest = drawn.shape.index(max(drawn.shape))
    neighbour = spot[:longest] + [(spot[longest] + 1) % drawn.shape[longest]] + spot[longest + 1:]
    return drawn.at[tuple(spot)].set(smallest).at[tuple(neighbour)].set(high)


def spiked(result, own_key, source, target, shards_of, factor):
    owner, partner = [(jnp.arange(result.shape[dim]) // (result.shape[dim] // shards_of)).reshape([-1 if axis == dim else 1 for axis in range(result.ndim)]) for dim in (source, target)]
    chosen = jax.random.permutation(own_key, shards_of)[partner]
    strong = (owner == chosen) | (owner == (partner + shards_of // 2) % shards_of)
    return jnp.where(strong, factor * result, result)


def steps_of(stream_key, shape, split, smallest, top_value):
    gain = 1.0
    for position, parts in split:
        heights = jax.random.uniform(jax.random.fold_in(jax.random.fold_in(stream_key, 6), position), (parts,), jnp.float32, smallest / len(split), top_value / len(split))
        gain = gain * jnp.repeat(jnp.exp(heights), shape[position] // parts).reshape((-1,) + (1,) * (len(shape) - 1 - position))
    return gain


def scatter_about(stream_key, shape, spread, reach, shards=(), held_as=jnp.bfloat16):
    array = jax.random.normal(stream_key, shape, jnp.float32) * spread
    if len(shards) > 0:
        array = steps_of(stream_key, shape, shards, -0.22, 0.18) * array
    return jnp.clip(array, min=-reach, max=reach).astype(held_as)


def bell_draw_with(key, dims, scale, reach, split, heavy, kind=jnp.bfloat16):
    entries = scale * jax.random.normal(key, dims, jnp.float32)
    if split:
        entries = entries * steps_of(key, dims, split, -0.22, 0.18)
    return jnp.clip(spiked(entries, jax.random.fold_in(key, 3), *heavy), -reach, reach).astype(kind)


def setup_inputs(seed: int = 0) -> dict:
    seeds = jax.random.split(jax.random.key(seed), 13)
    hot_rows = bell_draw_with(seeds[0], (DEVICES * HOT_CL * CLUSTER, D), 1.0, 6.0, ((0, 32),), (0, 1, 32, 2.75))
    cold_codes = jnp.clip(jax.random.uniform(seeds[1], (DEVICES * COLD_CL * CLUSTER, D), jnp.float32, -127.0, 127.0) * steps_of(seeds[1], (DEVICES * COLD_CL * CLUSTER, D), ((0, 32),), -0.4, 0.0), -127.0, 127.0).astype(jnp.bfloat16)
    scale_index = touch_ends(jax.random.randint(seeds[2], (DEVICES * COLD_CL * CLUSTER,), 0, NSCALE), jax.random.fold_in(seeds[2], 1), 0, NSCALE - 1).astype(jnp.int32)
    scale_table = jnp.clip(jnp.exp(jax.random.uniform(seeds[3], (NSCALE,), jnp.float32, math.log(0.004), math.log(0.04))), 0.004, 0.04)
    stale_rows = scatter_about(seeds[4], (DEVICES * BND_ROWS, D), 1.0, 6.0, ((0, 32),))
    tile_index = touch_ends(jax.random.randint(seeds[5], (DEVICES * CL, TILES), 0, SRC_CL), jax.random.fold_in(seeds[5], 1), 0, SRC_CL - 1).astype(jnp.int32)
    tile_count = touch_ends(jax.random.randint(seeds[6], (DEVICES * CL,), 1, TILES + 1), jax.random.fold_in(seeds[6], 1), 1, TILES).astype(jnp.int32)
    tile_values = scatter_about(seeds[7], (DEVICES * CL, TILES, CLUSTER, CLUSTER), (CLUSTER * TILES) ** -0.5, 0.3125, ((0, 32),))
    weight = scatter_about(seeds[8], (D, D), D ** -0.5, 0.1875, ((0, 8),))
    out_grad = scatter_about(seeds[9], (DEVICES * ROWS, D), 1.0, 6.0, ((0, 32),))
    stale_grads = scatter_about(seeds[10], (DEVICES * BND_ROWS, D), 1.0, 6.0, ((0, 32),))
    send_rows = touch_ends(jax.random.randint(seeds[11], (DEVICES * N_DOM, PEER_ROWS), 0, ROWS), jax.random.fold_in(seeds[11], 1), 0, ROWS - 1).astype(jnp.int32)
    return {"hot_rows": hot_rows, "cold_codes": cold_codes, "scale_index": scale_index, "scale_table": scale_table, "stale_rows": stale_rows, "tile_index": tile_index, "tile_count": tile_count, "tile_values": tile_values, "weight": weight, "out_grad": out_grad, "stale_grads": stale_grads, "send_rows": send_rows}


def dequantize(cold_codes, scale_index, scale_table):
    levels = jnp.arange(scale_table.shape[0], dtype=jnp.int32)
    lookup = jnp.sum(jnp.where(scale_index[:, None] == levels[None, :], scale_table[None, :], jnp.zeros_like(scale_table)[None, :]), axis=1)
    return (cold_codes.astype(jnp.float32) * lookup[:, None]).astype(jnp.bfloat16)


def silu_parts(preact):
    logistic = jax.nn.sigmoid(preact)
    return preact * logistic, logistic * (1.0 + preact * (1.0 - logistic))


def swap_peers(stacked):
    peer_rows = BND_ROWS // N_DOM
    blocks = stacked.reshape(N_GROUP, N_DOM, N_DOM, peer_rows, D)
    return jnp.swapaxes(blocks, 1, 2).reshape(DEVICES * BND_ROWS, D)


def reference(hot_rows, cold_codes, scale_index, scale_table, stale_rows, tile_index, tile_count, tile_values, weight, out_grad, stale_grads, send_rows):
    clusters_dev = HOT_CL + COLD_CL
    row_count = clusters_dev * CLUSTER
    src_count = clusters_dev + BND_ROWS // CLUSTER
    inputs = (hot_rows.reshape(DEVICES, HOT_CL * CLUSTER, D),
              cold_codes.reshape(DEVICES, COLD_CL * CLUSTER, D),
              scale_index.reshape(DEVICES, COLD_CL * CLUSTER),
              stale_rows.reshape(DEVICES, BND_ROWS, D),
              tile_index.reshape(DEVICES, clusters_dev, TILES),
              tile_count.reshape(DEVICES, clusters_dev),
              tile_values.reshape(DEVICES, clusters_dev, TILES, CLUSTER, CLUSTER),
              out_grad.reshape(DEVICES, row_count, D),
              stale_grads.reshape(DEVICES, BND_ROWS, D),
              send_rows.reshape(DEVICES, BND_ROWS))

    def device_step(running, pieces):
        hot, codes, indices, stale, tindex, tcount, tiles, grad_out, stale_back, sends = pieces
        local_rows = jnp.concatenate([hot, dequantize(codes, indices, scale_table)], axis=0)
        source = jnp.concatenate([local_rows, stale], axis=0).reshape(src_count, CLUSTER, D)
        live_mask = jnp.arange(TILES, dtype=jnp.int32)[None, :] < tcount[:, None]
        masked = jnp.where(live_mask[:, :, None, None], tiles, jnp.zeros_like(tiles))
        picked = jnp.take(source, tindex, axis=0)
        hidden = jnp.einsum('ckab,ckbd->cad', masked.astype(jnp.float32), picked.astype(jnp.float32))
        hidden = hidden.reshape(row_count, D).astype(jnp.bfloat16)
        preact = jnp.dot(hidden, weight, preferred_element_type=jnp.float32)
        activ, slope = silu_parts(preact)
        pre_grad = (grad_out.astype(jnp.float32) * slope).astype(jnp.bfloat16)
        partial_value = jnp.dot(hidden.T, pre_grad, preferred_element_type=jnp.float32)
        hid_grad = jnp.dot(pre_grad, weight.T, preferred_element_type=jnp.float32).astype(jnp.bfloat16)
        contrib = jnp.einsum('ckab,cad->ckbd', masked.astype(jnp.float32), hid_grad.reshape(clusters_dev, CLUSTER, D).astype(jnp.float32))
        onehot = (tindex.reshape(-1)[None, :] == jnp.arange(src_count, dtype=jnp.int32)[:, None]).astype(contrib.dtype)
        src_grad = jnp.dot(onehot, contrib.reshape(clusters_dev * TILES, CLUSTER * D), precision=lax.Precision.HIGHEST)
        src_grad = src_grad.reshape(src_count * CLUSTER, D)
        placing = (jnp.arange(row_count, dtype=jnp.int32)[:, None] == sends[None, :]).astype(jnp.bfloat16)
        returned = jnp.dot(placing, stale_back, preferred_element_type=jnp.float32)
        feature_grad = (src_grad[:row_count] + returned).astype(jnp.bfloat16)
        bound_grad = src_grad[row_count:].astype(jnp.bfloat16)
        outgoing = jnp.take(local_rows, sends, axis=0)
        return running + partial_value, (activ.astype(jnp.bfloat16), feature_grad, bound_grad, outgoing)

    start_grad = jnp.zeros((D, D), jnp.float32)
    weight_grad, stacked = lax.scan(device_step, start_grad, inputs)
    activ_all, feature_all, bound_all, outgoing_all = stacked
    activations = activ_all.reshape(DEVICES * row_count, D)
    feature_grad = feature_all.reshape(DEVICES * row_count, D)
    next_rows = swap_peers(outgoing_all)
    next_grads = swap_peers(bound_all)
    return activations, feature_grad, weight_grad, next_rows, next_grads
```

```python
import functools

import jax
import jax.numpy as jnp
from jax import lax
from jax.experimental import pallas as pl
from jax.experimental.pallas import tpu as pltpu
from jax.sharding import PartitionSpec as P

MESH = pl.DeviceIdType.MESH
F32, BF16 = jnp.float32, jnp.bfloat16
NT = (((1,), (1,)), ((), ()))


def each(lo, hi, body):
    if hi - lo <= 8:
        for i in range(lo, hi):
            body(i)
    else:
        pl.loop(lo, hi)(body)


def pieces(n_group, blk, depth):
    nc = min(n_group, depth // 128)
    sub = n_group // nc
    return nc, sub, blk // sub, depth // nc


def mm(a, b):
    return jnp.dot(a, b, preferred_element_type=F32)


def kernel(
    n_group, n_dom,
    tidx_ref, tcnt_ref, hot_ref, cold_ref, sidx_ref, table_ref, stale_ref, tile_ref, w_ref,
    og_ref, sg_ref, send_ref,
    act_ref, fg_ref, wg_ref, nr_ref, ng_ref,
    src, wbuf, hid, hid_t, pre, ptx, prx, own, stx, rrx, ztx, zrx, ftx, frx, acc, rowsf, outx, bgx,
    op_hi, op_lo, hgrad,
    ag_s, ag_r, pa_s, pa_r, nr_s, nr_r, ng_s, ng_r, pt_s, pt_r, st_s, st_r, z_s, z_r, f_s, f_r,
):
    g, d = lax.axis_index("group"), lax.axis_index("dom")
    n_pair = n_dom // 2
    pair, core = d // 2, d % 2
    partner = pair * 2 + (1 - core)
    blk, depth = w_ref.shape
    nc, sub, bs, cw = pieces(n_group, blk, depth)
    n_cl, slots, cl, _ = tile_ref.shape
    n_src = src.shape[0]
    rows = n_cl * cl
    peer = send_ref.shape[1]
    sends = n_dom * peer

    barrier = pltpu.get_barrier_semaphore()

    def hello_dom(r):
        pl.semaphore_signal(barrier, inc=1, device_id={"dom": (d + r) % n_dom}, device_id_type=MESH)

    def hello_group(r):
        pl.semaphore_signal(barrier, inc=1, device_id={"group": (g + r) % n_group}, device_id_type=MESH)

    each(1, n_dom, hello_dom)
    each(1, n_group, hello_group)
    pl.semaphore_wait(barrier, n_dom + n_group - 2)

    def remote(source, target, send_sem, recv_sem, where):
        return pltpu.make_async_remote_copy(
            src_ref=source, dst_ref=target, send_sem=send_sem, recv_sem=recv_sem,
            device_id=where, device_id_type=MESH)

    def chunk(i):
        return (g // sub + 1 + i) % nc

    def cols(ch):
        return pl.ds(pl.multiple_of(ch * cw, cw), cw)

    def ag_copy(ch, r):
        q = (pair + r) % n_pair
        return remote(w_ref.at[:, cols(ch)], wbuf.at[ch, d], ag_s.at[ch, r], ag_r.at[ch, r],
                      {"dom": q * 2 + core})

    def pa_first(ch):
        return remote(w_ref.at[:, cols(ch)], wbuf.at[ch, d], pa_s.at[ch, 0], pa_r.at[ch, 0],
                      {"dom": partner})

    def pa_copy(ch, r):
        slot = ((pair - r + n_pair) % n_pair) * 2 + core
        return remote(wbuf.at[ch, slot], wbuf.at[ch, slot], pa_s.at[ch, r], pa_r.at[ch, r],
                      {"dom": partner})

    for i in range(nc):
        each(1, n_pair, lambda r: ag_copy(chunk(i), r).start())
        pa_first(chunk(i)).start()
    for i in range(nc):
        wbuf[i, d] = w_ref[:, i * cw:(i + 1) * cw]

    spread = jnp.broadcast_to(sidx_ref[...].astype(F32), (cl, cl)).T
    scale = jnp.zeros((cl, 1), F32)
    for h in range(table_ref.shape[1] // cl):
        level = (lax.broadcasted_iota(jnp.int32, (cl, cl), 1) + h * cl).astype(F32)
        entry = jnp.broadcast_to(table_ref[:, h * cl:(h + 1) * cl], (cl, cl))
        scale = scale + jnp.sum(jnp.where(spread == level, entry, 0.0), axis=1, keepdims=True)
    src[0] = hot_ref[...]
    src[1] = (cold_ref[...].astype(F32) * scale).astype(BF16)
    src[2] = stale_ref[...]

    lift = (lax.broadcasted_iota(jnp.int32, (sends, n_dom), 0) // peer
            == lax.broadcasted_iota(jnp.int32, (sends, n_dom), 1)).astype(F32)
    wide = jnp.dot(lift, send_ref[...].astype(F32), precision=lax.Precision.HIGHEST,
                   preferred_element_type=F32)
    place = (lax.broadcasted_iota(jnp.int32, (sends, peer), 0) % peer
             == lax.broadcasted_iota(jnp.int32, (sends, peer), 1))
    listed = jnp.sum(jnp.where(place, wide, 0.0), axis=1, keepdims=True)
    picks = (listed == lax.broadcasted_iota(jnp.int32, (sends, rows), 1).astype(F32)).astype(F32)
    own_rows = jnp.concatenate([src[0], src[1]], axis=0)
    rowsf[...] = mm(picks.astype(BF16), own_rows)
    for p in range(n_dom):
        outx[p] = rowsf[p * peer:(p + 1) * peer, :].astype(BF16)
    nr_ref[d] = outx[d]

    def nr_copy(r):
        p = (d + r) % n_dom
        return remote(outx.at[p], nr_ref.at[d], nr_s.at[r], nr_r.at[r], {"dom": p})

    for c in range(n_cl):
        total = jnp.zeros((cl, depth), F32)
        for k in range(slots):
            tile = jnp.where(jnp.full((cl, cl), tcnt_ref[c], jnp.int32) > k, tile_ref[c, k], 0)
            total = total + mm(tile, src[tidx_ref[c, k]])
        hid[c * cl:(c + 1) * cl, :] = total.astype(BF16)
    turned = hid[...].astype(F32).T.astype(BF16)
    hid_t[...] = turned.reshape(n_pair, 2, blk, rows)
    for c in range(n_cl):
        for j in range(n_src):
            part = jnp.zeros((cl, cl), F32)
            for k in range(slots):
                live = (jnp.full((cl, cl), tcnt_ref[c], jnp.int32) > k) & (
                    jnp.full((cl, cl), tidx_ref[c, k], jnp.int32) == j)
                part = part + jnp.where(live, tile_ref[c, k].astype(F32), 0.0)
            part = part.T
            high = part.astype(BF16)
            op_hi[j, :, c * cl:(c + 1) * cl] = high
            op_lo[j, :, c * cl:(c + 1) * cl] = (part - high.astype(F32)).astype(BF16)

    def pt_copy(ch):
        return remote(ptx.at[ch], prx.at[ch], pt_s.at[ch], pt_r.at[ch], {"dom": partner})

    def st_copy(ch, r):
        q = (pair + r) % n_pair
        return remote(stx.at[ch, q], rrx.at[ch, r], st_s.at[ch, r], st_r.at[ch, r],
                      {"dom": q * 2 + core})

    def z_copy(r):
        to = (g + r) % n_group
        return remote(ztx.at[to // sub, to % sub], zrx.at[r], z_s.at[r], z_r.at[r], {"group": to})

    def f_copy(r):
        return remote(ftx, frx.at[r], f_s.at[r], f_r.at[r], {"group": (g + r) % n_group})

    def stage_a(i):
        ch = chunk(i)

        def relay(r):
            ag_copy(ch, r).wait_recv()
            pa_copy(ch, r).start()

        each(1, n_pair, relay)
        pa_first(ch).wait_recv()
        each(1, n_pair, lambda r: pa_copy(ch, r).wait_recv())
        weight = wbuf[ch].reshape(depth, cw)
        preact = mm(hid[...], weight)
        s = jax.nn.sigmoid(preact)
        act_ref[:, cols(ch)] = (preact * s).astype(BF16)
        slope = s * (1.0 + preact * (1.0 - s))
        pg = (og_ref[:, cols(ch)].astype(F32) * slope).astype(BF16)
        pre[ch] = pg
        away = mm(hid_t[:, 1 - core].reshape(n_pair * blk, rows), pg)
        ptx[ch] = away.astype(BF16).reshape(n_pair, blk, cw)
        pt_copy(ch).start()
        here = mm(hid_t[:, core].reshape(n_pair * blk, rows), pg)
        own[ch] = here.reshape(n_pair, blk, cw)

    def stage_b(i):
        ch = chunk(i)
        pt_copy(ch).wait_recv()
        stx[ch] = (own[ch] + prx[ch].astype(F32)).astype(BF16)
        each(1, n_pair, lambda r: st_copy(ch, r).start())
        acc[i] = (own[ch, pair] + prx[ch, pair].astype(F32)).reshape(sub, bs, cw)

    def stage_c(i):
        ch = chunk(i)

        def add(r):
            st_copy(ch, r).wait_recv()
            acc[i] = acc[i] + rrx[ch, r].astype(F32).reshape(sub, bs, cw)

        each(1, n_pair, add)
        ztx[ch] = acc[i].astype(BF16)
        for h in range(sub):
            if i < nc - 1:
                z_copy((ch * sub + h - g + n_group) % n_group).start()
            elif h > 0:
                mate = ch * sub + (g + h) % sub
                z_copy((mate - g + n_group) % n_group).start()

    for i in range(nc):
        stage_a(i)
        if i >= 1:
            stage_b(i - 1)
        if i == 0:
            each(1, n_dom, lambda r: nr_copy(r).start())
        if i >= 2:
            stage_c(i - 2)

    def back(m):
        part = jnp.zeros((rows, cw), F32)
        for c in range(nc):
            wpart = wbuf[c].reshape(depth, cw)[m * cw:(m + 1) * cw]
            part = part + lax.dot_general(pre[c], wpart, NT, preferred_element_type=F32)
        hgrad[:, m * cw:(m + 1) * cw] = part.astype(BF16)

    for m in range(nc):
        back(m)
        if m == 0:
            stage_b(nc - 1)

    def source_grad(j):
        return mm(op_hi[j], hgrad[...]) + mm(op_lo[j], hgrad[...])

    rowsf[...] = source_grad(n_src - 1)
    for p in range(n_dom):
        bgx[p] = rowsf[p * peer:(p + 1) * peer, :].astype(BF16)
    ng_ref[d] = bgx[d]

    def ng_copy(r):
        p = (d + r) % n_dom
        return remote(bgx.at[p], ng_ref.at[d], ng_s.at[r], ng_r.at[r], {"dom": p})

    each(1, n_dom, lambda r: ng_copy(r).start())
    if nc >= 2:
        stage_c(nc - 2)
    stage_c(nc - 1)

    def gather(r):
        z_copy(r).wait_recv()
        acc[nc - 1, g % sub] = acc[nc - 1, g % sub] + zrx[r].astype(F32)

    each(1, n_group, gather)
    ftx[...] = acc[nc - 1, g % sub].astype(BF16)
    each(1, n_group, lambda r: f_copy(r).start())

    def store(owner, value):
        wg_ref[pl.ds(pl.multiple_of(owner % sub * bs, bs), bs), cols(owner // sub)] = value.astype(F32)

    store(g, ftx[...])

    for j in range(n_src - 1):
        back_rows = lax.dot_general(
            picks[:, j * cl:(j + 1) * cl].T.astype(BF16), sg_ref[...], (((1,), (0,)), ((), ())),
            preferred_element_type=F32)
        fg_ref[j * cl:(j + 1) * cl, :] = (source_grad(j) + back_rows).astype(BF16)

    def take(r):
        f_copy(r).wait_recv()
        store((g - r + n_group) % n_group, frx[r])

    each(1, n_group, take)

    def drain_dom(r):
        nr_copy(r).wait()
        ng_copy(r).wait()

    each(1, n_dom, drain_dom)
    for i in range(nc):
        ch = chunk(i)

        def drain(r):
            ag_copy(ch, r).wait_send()
            pa_copy(ch, r).wait_send()
            st_copy(ch, r).wait_send()

        each(1, n_pair, drain)
        pa_first(ch).wait_send()
        pt_copy(ch).wait_send()

    def drain_group(r):
        z_copy(r).wait_send()
        f_copy(r).wait_send()

    each(1, n_group, drain_group)


def local(n_group, n_dom, hot_rows, cold_codes, scale_index, scale_table, stale_rows, tile_index,
          tile_count, tile_values, weight, out_grad, stale_grads, send_rows):
    blk, depth = weight.shape
    rows = out_grad.shape[0]
    cl = tile_values.shape[2]
    peer = send_rows.shape[1]
    n_pair = n_dom // 2
    nc, sub, bs, cw = pieces(n_group, blk, depth)
    n_src = rows // cl + stale_rows.shape[0] // cl
    vmem, smem = pl.BlockSpec(memory_space=pltpu.VMEM), pl.BlockSpec(memory_space=pltpu.SMEM)
    dma = pltpu.SemaphoreType.DMA
    out = pl.pallas_call(
        functools.partial(kernel, n_group, n_dom),
        out_shape=(
            jax.ShapeDtypeStruct((rows, depth), BF16),
            jax.ShapeDtypeStruct((rows, depth), BF16),
            jax.ShapeDtypeStruct((blk, depth), F32),
            jax.ShapeDtypeStruct((n_dom, peer, depth), BF16),
            jax.ShapeDtypeStruct((n_dom, peer, depth), BF16),
        ),
        in_specs=[smem] * 2 + [vmem] * 10,
        out_specs=(vmem,) * 5,
        scratch_shapes=[
            pltpu.VMEM((n_src, cl, depth), BF16),
            pltpu.VMEM((nc, n_dom, blk, cw), BF16),
            pltpu.VMEM((rows, depth), BF16),
            pltpu.VMEM((n_pair, 2, blk, rows), BF16),
            pltpu.VMEM((nc, rows, cw), BF16),
            pltpu.VMEM((nc, n_pair, blk, cw), BF16),
            pltpu.VMEM((nc, n_pair, blk, cw), BF16),
            pltpu.VMEM((nc, n_pair, blk, cw), F32),
            pltpu.VMEM((nc, n_pair, blk, cw), BF16),
            pltpu.VMEM((nc, n_pair, blk, cw), BF16),
            pltpu.VMEM((nc, sub, bs, cw), BF16),
            pltpu.VMEM((n_group, bs, cw), BF16),
            pltpu.VMEM((bs, cw), BF16),
            pltpu.VMEM((n_group, bs, cw), BF16),
            pltpu.VMEM((nc, sub, bs, cw), F32),
            pltpu.VMEM((n_dom * peer, depth), F32),
            pltpu.VMEM((n_dom, peer, depth), BF16),
            pltpu.VMEM((n_dom, peer, depth), BF16),
            pltpu.VMEM((n_src, cl, rows), BF16),
            pltpu.VMEM((n_src, cl, rows), BF16),
            pltpu.VMEM((rows, depth), BF16),
            dma((nc, n_pair)), dma((nc, n_pair)), dma((nc, n_pair)), dma((nc, n_pair)),
            dma((n_dom,)), dma((n_dom,)), dma((n_dom,)), dma((n_dom,)),
            dma((nc,)), dma((nc,)), dma((nc, n_pair)), dma((nc, n_pair)),
            dma((n_group,)), dma((n_group,)), dma((n_group,)), dma((n_group,)),
        ],
        compiler_params=pltpu.CompilerParams(
            collective_id=0, has_side_effects=True, vmem_limit_bytes=48 * 1024 * 1024),
    )(tile_index, tile_count, hot_rows, cold_codes, scale_index.reshape(1, -1),
      scale_table.reshape(1, -1), stale_rows, tile_values, weight, out_grad, stale_grads, send_rows)
    act, fg, wg, nr, ng = out
    return act, fg, wg, nr.reshape(-1, depth), ng.reshape(-1, depth)


def solution(mesh):
    both = ("group", "dom")
    return jax.shard_map(
        functools.partial(local, mesh.shape["group"], mesh.shape["dom"]),
        mesh=mesh,
        in_specs=(
            P(both, None), P(both, None), P(both), P(), P(both, None), P(both, None), P(both),
            P(both, None, None, None), P("dom", None), P(both, None), P(both, None), P(both, None),
        ),
        out_specs=(P(both, None), P(both, None), P("dom", None), P(both, None), P(both, None)),
        check_vma=False,
    )
```

```python
import functools

import jax
import jax.numpy as jnp
from jax import lax
from jax.experimental import pallas as pl
from jax.experimental.pallas import tpu as pltpu
from jax.sharding import PartitionSpec as P

MESH = pl.DeviceIdType.MESH
F32, BF16 = jnp.float32, jnp.bfloat16
NT = (((1,), (1,)), ((), ()))


def each(lo, hi, body):
    if hi - lo <= 8:
        for i in range(lo, hi):
            body(i)
    else:
        pl.loop(lo, hi)(body)


def pieces(n_group, blk, depth):
    nc = min(n_group, depth // 128)
    sub = n_group // nc
    return nc, sub, blk // sub, depth // nc


def flip(value, mask):
    bit = 1
    while bit <= mask:
        if mask & bit:
            value = value + bit - 2 * bit * (value // bit % 2)
        bit *= 2
    return value


def mm(a, b):
    return jnp.dot(a, b, preferred_element_type=F32)


def kernel(
    n_group, n_dom,
    tidx_hbm, tcnt_hbm, hot_hbm, cold_hbm, sidx_hbm, table_hbm, stale_hbm, tile_hbm, w_ref,
    og_hbm, sg_hbm, send_hbm,
    act_ref, fg_ref, wg_ref, nr_ref, ng_ref,
    tidx_ref, tcnt_ref, cold_ref, sidx_ref, table_ref, tile_ref, og_ref, sg_ref, send_ref,
    src, wbuf, hid, hid_t, pre, ptx, prx, own, work, stx, rrx, ztx, zrx, ftx, frx, acc, rowsf, outx,
    bgx, op_hi, op_lo, hgrad,
    in_s, own_s, ag_s, ag_r, pa_s, pa_r, nr_s, nr_r, ng_s, ng_r, pt_s, pt_r, st_s, st_r, z_s, z_r,
    f_s, f_r,
):
    g, d = lax.axis_index("group"), lax.axis_index("dom")
    n_pair = n_dom // 2
    pair, core = d // 2, d % 2
    partner = pair * 2 + (1 - core)
    blk, depth = w_ref.shape
    nc, sub, bs, cw = pieces(n_group, blk, depth)
    n_cl, slots, cl, _ = tile_ref.shape
    n_src = src.shape[0]
    rows = n_cl * cl
    peer = send_ref.shape[1]
    sends = n_dom * peer

    bits = n_pair.bit_length() - 1

    loads = [pltpu.make_async_copy(a, b, in_s.at[n]) for n, (a, b) in enumerate((
        (hot_hbm, src.at[0]), (cold_hbm, cold_ref), (stale_hbm, src.at[2]), (sidx_hbm, sidx_ref),
        (table_hbm, table_ref), (send_hbm, send_ref), (tile_hbm, tile_ref), (tidx_hbm, tidx_ref),
        (tcnt_hbm, tcnt_ref), (og_hbm, og_ref), (sg_hbm, sg_ref)))]
    for load in loads:
        load.start()
    barrier = pltpu.get_barrier_semaphore()

    def hello_dom(r):
        pl.semaphore_signal(barrier, inc=1, device_id={"dom": (d + r) % n_dom}, device_id_type=MESH)

    def hello_group(r):
        pl.semaphore_signal(barrier, inc=1, device_id={"group": (g + r) % n_group}, device_id_type=MESH)

    each(1, n_dom, hello_dom)
    each(1, n_group, hello_group)
    pl.semaphore_wait(barrier, n_dom + n_group - 2)

    def remote(source, target, send_sem, recv_sem, where):
        return pltpu.make_async_remote_copy(
            src_ref=source, dst_ref=target, send_sem=send_sem, recv_sem=recv_sem,
            device_id=where, device_id_type=MESH)

    def chunk(i):
        return (g // sub + 1 + i) % nc

    def cols(ch):
        return pl.ds(pl.multiple_of(ch * cw, cw), cw)

    def axis(i, t):
        return 1 << ((t + i) % bits)

    def near(i, r):
        return flip(pair, sum(axis(i, t) for t in range(bits) if r >> t & 1))

    def ag_copy(i, r):
        t = r.bit_length() - 1
        slot = near(i, r - (1 << t)) * 2 + core
        source = w_ref.at[:, cols(chunk(i))] if r == 1 << t else wbuf.at[chunk(i), slot]
        return remote(source, wbuf.at[chunk(i), slot], ag_s.at[i, r], ag_r.at[i, r],
                      {"dom": near(i, 1 << t) * 2 + core})

    def pa_copy(i, r):
        slot = near(i, r) * 2 + core
        source = w_ref.at[:, cols(chunk(i))] if r == 0 else wbuf.at[chunk(i), slot]
        return remote(source, wbuf.at[chunk(i), slot], pa_s.at[i, r], pa_r.at[i, r],
                      {"dom": partner})

    def keep(i):
        return pltpu.make_async_copy(w_ref.at[:, cols(chunk(i))], wbuf.at[chunk(i), d], own_s.at[i])

    for i in range(nc):
        ag_copy(i, 1).start()
    for i in range(nc):
        for t in range(1, bits):
            ag_copy(i, 1 << t).start()
        pa_copy(i, 0).start()
        keep(i).start()
    for load in loads[:9]:
        load.wait()

    def relay(i):
        for r in range(1, n_pair):
            ag_copy(i, r).wait_recv()
            pa_copy(i, r).start()
            for t in range(r.bit_length(), bits):
                ag_copy(i, r + (1 << t)).start()

    spread = jnp.broadcast_to(sidx_ref[...].astype(F32), (cl, cl)).T
    scale = jnp.zeros((cl, 1), F32)
    for h in range(table_ref.shape[1] // cl):
        level = (lax.broadcasted_iota(jnp.int32, (cl, cl), 1) + h * cl).astype(F32)
        entry = jnp.broadcast_to(table_ref[:, h * cl:(h + 1) * cl], (cl, cl))
        scale = scale + jnp.sum(jnp.where(spread == level, entry, 0.0), axis=1, keepdims=True)
    src[1] = (cold_ref[...].astype(F32) * scale).astype(BF16)

    lift = (lax.broadcasted_iota(jnp.int32, (sends, n_dom), 0) // peer
            == lax.broadcasted_iota(jnp.int32, (sends, n_dom), 1)).astype(F32)
    wide = jnp.dot(lift, send_ref[...].astype(F32), precision=lax.Precision.HIGHEST,
                   preferred_element_type=F32)
    place = (lax.broadcasted_iota(jnp.int32, (sends, peer), 0) % peer
             == lax.broadcasted_iota(jnp.int32, (sends, peer), 1))
    listed = jnp.sum(jnp.where(place, wide, 0.0), axis=1, keepdims=True)
    picks = (listed == lax.broadcasted_iota(jnp.int32, (sends, rows), 1).astype(F32)).astype(F32)
    own_rows = jnp.concatenate([src[0], src[1]], axis=0)
    rowsf[...] = mm(picks.astype(BF16), own_rows)
    for p in range(n_dom):
        outx[p] = rowsf[p * peer:(p + 1) * peer, :].astype(BF16)
    nr_ref[d] = outx[d]

    def nr_copy(r):
        p = (d + r) % n_dom
        return remote(outx.at[p], nr_ref.at[d], nr_s.at[r], nr_r.at[r], {"dom": p})

    relay(0)

    for c in range(n_cl):
        total = jnp.zeros((cl, depth), F32)
        for k in range(slots):
            tile = jnp.where(jnp.full((cl, cl), tcnt_ref[c], jnp.int32) > k, tile_ref[c, k], 0)
            total = total + mm(tile, src[tidx_ref[c, k]])
        hid[c * cl:(c + 1) * cl, :] = total.astype(BF16)
    turned = hid[...].astype(F32).T.astype(BF16)
    hid_t[...] = turned.reshape(n_pair, 2, blk, rows)
    for c in range(n_cl):
        for j in range(n_src):
            part = jnp.zeros((cl, cl), F32)
            for k in range(slots):
                live = (jnp.full((cl, cl), tcnt_ref[c], jnp.int32) > k) & (
                    jnp.full((cl, cl), tidx_ref[c, k], jnp.int32) == j)
                part = part + jnp.where(live, tile_ref[c, k].astype(F32), 0.0)
            part = part.T
            high = part.astype(BF16)
            op_hi[j, :, c * cl:(c + 1) * cl] = high
            op_lo[j, :, c * cl:(c + 1) * cl] = (part - high.astype(F32)).astype(BF16)

    def pt_copy(ch):
        return remote(ptx.at[ch], prx.at[ch], pt_s.at[ch], pt_r.at[ch], {"dom": partner})

    def st_copy(i, r):
        low = r & -r
        return remote(stx.at[i, r], rrx.at[i, r], st_s.at[i, r], st_r.at[i, r],
                      {"dom": near(i, low) * 2 + core})

    def z_copy(r):
        to = (g + r) % n_group
        return remote(ztx.at[to // sub, to % sub], zrx.at[r], z_s.at[r], z_r.at[r], {"group": to})

    def f_copy(r):
        return remote(ftx, frx.at[r], f_s.at[r], f_r.at[r], {"group": (g + r) % n_group})

    def stage_a(i):
        ch = chunk(i)
        if i + 1 < nc:
            relay(i + 1)
        keep(i).wait()
        for r in range(n_pair):
            pa_copy(i, r).wait_recv()
        weight = wbuf[ch].reshape(depth, cw)
        if i == 0:
            loads[9].wait()
        preact = mm(hid[...], weight)
        s = jax.nn.sigmoid(preact)
        act_ref[:, cols(ch)] = (preact * s).astype(BF16)
        slope = s * (1.0 + preact * (1.0 - s))
        pg = (og_ref[:, cols(ch)].astype(F32) * slope).astype(BF16)
        pre[ch] = pg
        away = mm(hid_t[:, 1 - core].reshape(n_pair * blk, rows), pg)
        ptx[ch] = away.astype(BF16).reshape(n_pair, blk, cw)
        pt_copy(ch).start()
        here = mm(hid_t[:, core].reshape(n_pair * blk, rows), pg)
        own[ch] = here.reshape(n_pair, blk, cw)

    def stage_b(i):
        ch = chunk(i)
        pt_copy(ch).wait_recv()
        for r in [*range(1, n_pair, 2), *range(0, n_pair, 2)]:
            q = near(i, r)
            both = own[ch, q] + prx[ch, q].astype(F32)
            if r % 2:
                stx[i, r] = both.astype(BF16)
                st_copy(i, r).start()
            else:
                work[i, r] = both

    def stage_fold(i, t):
        step, after = 1 << t, 2 << t
        for r in [*range(after, n_pair, 2 * after), *range(0, n_pair, 2 * after)]:
            st_copy(i, r + step).wait_recv()
            both = work[i, r] + rrx[i, r + step].astype(F32)
            if r:
                stx[i, r] = both.astype(BF16)
                st_copy(i, r).start()
            else:
                work[i, r] = both

    def stage_c(i):
        ch = chunk(i)
        last = n_pair // 2
        st_copy(i, last).wait_recv()
        acc[i] = (work[i, 0] + rrx[i, last].astype(F32)).reshape(sub, bs, cw)
        ztx[ch] = acc[i].astype(BF16)
        for h in range(sub):
            if i < nc - 1:
                z_copy((ch * sub + h - g + n_group) % n_group).start()
            elif h > 0:
                mate = ch * sub + (g + h) % sub
                z_copy((mate - g + n_group) % n_group).start()

    def step(n):
        if n == 0:
            each(1, n_dom, lambda r: nr_copy(r).start())
        for t in range(-1, bits):
            i = n - 2 - t
            if 0 <= i < nc:
                if t < 0:
                    stage_b(i)
                elif t < bits - 1:
                    stage_fold(i, t)
                else:
                    stage_c(i)

    for i in range(nc):
        stage_a(i)
        if i == 1:
            loads[10].wait()
        step(i)

    def back(m):
        part = jnp.zeros((rows, cw), F32)
        for c in range(nc):
            wpart = wbuf[c].reshape(depth, cw)[m * cw:(m + 1) * cw]
            part = part + lax.dot_general(pre[c], wpart, NT, preferred_element_type=F32)
        hgrad[:, m * cw:(m + 1) * cw] = part.astype(BF16)

    late = nc
    for m in range(nc):
        back(m)
        if m == nc // 2 - 1:
            step(late)

    def source_grad(j):
        return mm(op_hi[j], hgrad[...]) + mm(op_lo[j], hgrad[...])

    rowsf[...] = source_grad(n_src - 1)
    for p in range(n_dom):
        bgx[p] = rowsf[p * peer:(p + 1) * peer, :].astype(BF16)
    ng_ref[d] = bgx[d]

    def ng_copy(r):
        p = (d + r) % n_dom
        return remote(bgx.at[p], ng_ref.at[d], ng_s.at[r], ng_r.at[r], {"dom": p})

    each(1, n_dom, lambda r: ng_copy(r).start())
    for n in range(nc + 1, nc + 1 + bits):
        step(n)

    def gather(r):
        z_copy(r).wait_recv()
        acc[nc - 1, g % sub] = acc[nc - 1, g % sub] + zrx[r].astype(F32)

    each(1, n_group, gather)
    ftx[...] = acc[nc - 1, g % sub].astype(BF16)
    each(1, n_group, lambda r: f_copy(r).start())

    def store(owner, value):
        wg_ref[pl.ds(pl.multiple_of(owner % sub * bs, bs), bs), cols(owner // sub)] = value.astype(F32)

    store(g, ftx[...])

    for j in range(n_src - 1):
        back_rows = lax.dot_general(
            picks[:, j * cl:(j + 1) * cl].T.astype(BF16), sg_ref[...], (((1,), (0,)), ((), ())),
            preferred_element_type=F32)
        fg_ref[j * cl:(j + 1) * cl, :] = (source_grad(j) + back_rows).astype(BF16)

    def take(r):
        f_copy(r).wait_recv()
        store((g - r + n_group) % n_group, frx[r])

    each(1, n_group, take)

    def drain_dom(r):
        nr_copy(r).wait()
        ng_copy(r).wait()

    each(1, n_dom, drain_dom)
    for i in range(nc):
        ch = chunk(i)

        def drain(r):
            ag_copy(i, r).wait_send()
            pa_copy(i, r).wait_send()
            st_copy(i, r).wait_send()

        for r in range(1, n_pair):
            drain(r)
        pa_copy(i, 0).wait_send()
        pt_copy(ch).wait_send()

    def drain_group(r):
        z_copy(r).wait_send()
        f_copy(r).wait_send()

    each(1, n_group, drain_group)


def write_out(*refs):
    sems = refs[10]
    copies = [pltpu.make_async_copy(refs[n], refs[5 + n], sems.at[n]) for n in range(5)]
    for copy in copies:
        copy.start()
    for copy in copies:
        copy.wait()


def local(n_group, n_dom, hot_rows, cold_codes, scale_index, scale_table, stale_rows, tile_index,
          tile_count, tile_values, weight, out_grad, stale_grads, send_rows):
    blk, depth = weight.shape
    rows = out_grad.shape[0]
    cl = tile_values.shape[2]
    peer = send_rows.shape[1]
    n_pair = n_dom // 2
    nc, sub, bs, cw = pieces(n_group, blk, depth)
    n_src = rows // cl + stale_rows.shape[0] // cl
    vmem, hbm = pl.BlockSpec(memory_space=pltpu.VMEM), pl.BlockSpec(memory_space=pltpu.HBM)
    dma = pltpu.SemaphoreType.DMA
    out = pl.pallas_call(
        functools.partial(kernel, n_group, n_dom),
        out_shape=(
            jax.ShapeDtypeStruct((rows, depth), BF16),
            jax.ShapeDtypeStruct((rows, depth), BF16),
            jax.ShapeDtypeStruct((blk, depth), F32),
            jax.ShapeDtypeStruct((n_dom, peer, depth), BF16),
            jax.ShapeDtypeStruct((n_dom, peer, depth), BF16),
        ),
        in_specs=[hbm] * 12,
        out_specs=(vmem,) * 5,
        scratch_shapes=[
            pltpu.SMEM(tile_index.shape, jnp.int32),
            pltpu.SMEM(tile_count.shape, jnp.int32),
            pltpu.VMEM(cold_codes.shape, BF16),
            pltpu.VMEM((1, scale_index.shape[0]), jnp.int32),
            pltpu.VMEM((1, scale_table.shape[0]), F32),
            pltpu.VMEM(tile_values.shape, BF16),
            pltpu.VMEM(out_grad.shape, BF16),
            pltpu.VMEM(stale_grads.shape, BF16),
            pltpu.VMEM(send_rows.shape, jnp.int32),
            pltpu.VMEM((n_src, cl, depth), BF16),
            pltpu.VMEM((nc, n_dom, blk, cw), BF16),
            pltpu.VMEM((rows, depth), BF16),
            pltpu.VMEM((n_pair, 2, blk, rows), BF16),
            pltpu.VMEM((nc, rows, cw), BF16),
            pltpu.VMEM((nc, n_pair, blk, cw), BF16),
            pltpu.VMEM((nc, n_pair, blk, cw), BF16),
            pltpu.VMEM((nc, n_pair, blk, cw), F32),
            pltpu.VMEM((nc, n_pair, blk, cw), F32),
            pltpu.VMEM((nc, n_pair, blk, cw), BF16),
            pltpu.VMEM((nc, n_pair, blk, cw), BF16),
            pltpu.VMEM((nc, sub, bs, cw), BF16),
            pltpu.VMEM((n_group, bs, cw), BF16),
            pltpu.VMEM((bs, cw), BF16),
            pltpu.VMEM((n_group, bs, cw), BF16),
            pltpu.VMEM((nc, sub, bs, cw), F32),
            pltpu.VMEM((n_dom * peer, depth), F32),
            pltpu.VMEM((n_dom, peer, depth), BF16),
            pltpu.VMEM((n_dom, peer, depth), BF16),
            pltpu.VMEM((n_src, cl, rows), BF16),
            pltpu.VMEM((n_src, cl, rows), BF16),
            pltpu.VMEM((rows, depth), BF16),
            dma((11,)), dma((nc,)),
            dma((nc, n_pair)), dma((nc, n_pair)), dma((nc, n_pair)), dma((nc, n_pair)),
            dma((n_dom,)), dma((n_dom,)), dma((n_dom,)), dma((n_dom,)),
            dma((nc,)), dma((nc,)), dma((nc, n_pair)), dma((nc, n_pair)),
            dma((n_group,)), dma((n_group,)), dma((n_group,)), dma((n_group,)),
        ],
        compiler_params=pltpu.CompilerParams(
            collective_id=0, has_side_effects=True, vmem_limit_bytes=48 * 1024 * 1024),
    )(*[pltpu.with_memory_space_constraint(a, pltpu.HBM) for a in (
        tile_index, tile_count, hot_rows, cold_codes, scale_index.reshape(1, -1),
        scale_table.reshape(1, -1), stale_rows, tile_values, weight, out_grad, stale_grads,
        send_rows)])
    act, fg, wg, nr, ng = pl.pallas_call(
        write_out,
        out_shape=tuple(jax.ShapeDtypeStruct(o.shape, o.dtype) for o in out),
        in_specs=[vmem] * 5,
        out_specs=(hbm,) * 5,
        scratch_shapes=[dma((5,))],
        compiler_params=pltpu.CompilerParams(vmem_limit_bytes=8 * 1024 * 1024),
    )(*out)
    return act, fg, wg, nr.reshape(-1, depth), ng.reshape(-1, depth)


def solution(mesh):
    both = ("group", "dom")
    return jax.shard_map(
        functools.partial(local, mesh.shape["group"], mesh.shape["dom"]),
        mesh=mesh,
        in_specs=(
            P(both, None), P(both, None), P(both), P(), P(both, None), P(both, None), P(both),
            P(both, None, None, None), P("dom", None), P(both, None), P(both, None), P(both, None),
        ),
        out_specs=(P(both, None), P(both, None), P("dom", None), P(both, None), P(both, None)),
        check_vma=False,
    )
```

```python
import functools

import jax
import jax.numpy as jnp
from jax import lax
from jax.experimental import pallas as pl
from jax.experimental.pallas import tpu as pltpu
from jax.sharding import PartitionSpec as P

MESH = pl.DeviceIdType.MESH
F32, BF16 = jnp.float32, jnp.bfloat16
NT = (((1,), (1,)), ((), ()))


def each(lo, hi, body):
    if hi - lo <= 8:
        for i in range(lo, hi):
            body(i)
    else:
        pl.loop(lo, hi)(body)


def pieces(n_group, blk, depth):
    nc = min(n_group, depth // 128)
    sub = n_group // nc
    return nc, sub, blk // sub, depth // nc


def flip(value, mask):
    bit = 1
    while bit <= mask:
        if mask & bit:
            value = value + bit - 2 * bit * (value // bit % 2)
        bit *= 2
    return value


def mm(a, b):
    return jnp.dot(a, b, preferred_element_type=F32)


def kernel(
    n_group, n_dom,
    tidx_hbm, tcnt_hbm, hot_hbm, cold_hbm, sidx_hbm, table_hbm, stale_hbm, tile_hbm, w_ref,
    og_hbm, sg_hbm, send_hbm,
    act_ref, fg_ref, wg_ref, nr_ref, ng_ref,
    tidx_ref, tcnt_ref, cold_ref, sidx_ref, table_ref, tile_ref, og_ref, sg_ref, send_ref,
    src, wbuf, hid, hid_t, pre, ptx, prx, own, work, stx, rrx, ztx, zrx, ftx, frx, acc, rowsf, outx,
    bgx, op_hi, op_lo, hgrad,
    in_s, own_s, ag_s, ag_r, zw_s, zw_r, pa_s, pa_r, nr_s, nr_r, ng_s, ng_r, pt_s, pt_r, st_s, st_r, z_s, z_r,
    f_s, f_r,
):
    g, d = lax.axis_index("group"), lax.axis_index("dom")
    n_pair = n_dom // 2
    pair, core = d // 2, d % 2
    partner = pair * 2 + (1 - core)
    blk, depth = w_ref.shape
    nc, sub, bs, cw = pieces(n_group, blk, depth)
    n_cl, slots, cl, _ = tile_ref.shape
    n_src = src.shape[0]
    rows = n_cl * cl
    peer = send_ref.shape[1]
    sends = n_dom * peer

    bits = n_pair.bit_length() - 1

    loads = [pltpu.make_async_copy(a, b, in_s.at[n]) for n, (a, b) in enumerate((
        (hot_hbm, src.at[0]), (cold_hbm, cold_ref), (stale_hbm, src.at[2]), (sidx_hbm, sidx_ref),
        (table_hbm, table_ref), (send_hbm, send_ref), (tile_hbm, tile_ref), (tidx_hbm, tidx_ref),
        (tcnt_hbm, tcnt_ref), (og_hbm, og_ref), (sg_hbm, sg_ref)))]
    for load in loads:
        load.start()
    barrier = pltpu.get_barrier_semaphore()

    def hello_dom(r):
        pl.semaphore_signal(barrier, inc=1, device_id={"dom": (d + r) % n_dom}, device_id_type=MESH)

    def hello_group(r):
        pl.semaphore_signal(barrier, inc=1, device_id={"group": (g + r) % n_group}, device_id_type=MESH)

    each(1, n_dom, hello_dom)
    each(1, n_group, hello_group)
    pl.semaphore_wait(barrier, n_dom + n_group - 2)

    def remote(source, target, send_sem, recv_sem, where):
        return pltpu.make_async_remote_copy(
            src_ref=source, dst_ref=target, send_sem=send_sem, recv_sem=recv_sem,
            device_id=where, device_id_type=MESH)

    def chunk(i):
        return flip(g // sub, (i + 1) % nc)

    def cols(ch):
        return pl.ds(pl.multiple_of(ch * cw, cw), cw)

    def axis(i, t):
        return 1 << t

    def near(i, r):
        return flip(pair, sum(axis(i, t) for t in range(bits) if r >> t & 1))

    def ag_copy(i, r):
        return remote(w_ref.at[:, cols(chunk(i))], wbuf.at[chunk(i), d], ag_s.at[i, r],
                      ag_r.at[i, r], {"dom": near(i, r) * 2 + core})

    def zw_copy(r):
        slot = near(0, r) * 2 + core
        return remote(wbuf.at[chunk(0), slot], wbuf.at[chunk(0), slot], zw_s.at[r], zw_r.at[r],
                      {"group": flip(g, sub)})

    def zw_in(r):
        slot = near(0, r) * 2 + core
        return remote(wbuf.at[chunk(nc - 1), slot], wbuf.at[chunk(nc - 1), slot], zw_s.at[r],
                      zw_r.at[r], {"group": flip(g, sub)})

    def pa_copy(i, r):
        slot = near(i, r) * 2 + core
        source = w_ref.at[:, cols(chunk(i))] if r == 0 else wbuf.at[chunk(i), slot]
        return remote(source, wbuf.at[chunk(i), slot], pa_s.at[i, r], pa_r.at[i, r],
                      {"dom": partner})

    def keep(i):
        return pltpu.make_async_copy(w_ref.at[:, cols(chunk(i))], wbuf.at[chunk(i), d], own_s.at[i])

    for i in range(nc - 1):
        for r in range(1, n_pair):
            ag_copy(i, r).start()
    for i in range(nc):
        pa_copy(i, 0).start()
        keep(i).start()
    for load in loads[:9]:
        load.wait()

    def relay(i):
        for r in range(1, n_pair):
            if i < nc - 1:
                ag_copy(i, r).wait_recv()
            else:
                zw_in(r).wait_recv()
            if i == 0:
                zw_copy(r).start()
            pa_copy(i, r).start()

    spread = jnp.broadcast_to(sidx_ref[...].astype(F32), (cl, cl)).T
    scale = jnp.zeros((cl, 1), F32)
    for h in range(table_ref.shape[1] // cl):
        level = (lax.broadcasted_iota(jnp.int32, (cl, cl), 1) + h * cl).astype(F32)
        entry = jnp.broadcast_to(table_ref[:, h * cl:(h + 1) * cl], (cl, cl))
        scale = scale + jnp.sum(jnp.where(spread == level, entry, 0.0), axis=1, keepdims=True)
    src[1] = (cold_ref[...].astype(F32) * scale).astype(BF16)

    lift = (lax.broadcasted_iota(jnp.int32, (sends, n_dom), 0) // peer
            == lax.broadcasted_iota(jnp.int32, (sends, n_dom), 1)).astype(F32)
    wide = jnp.dot(lift, send_ref[...].astype(F32), precision=lax.Precision.HIGHEST,
                   preferred_element_type=F32)
    place = (lax.broadcasted_iota(jnp.int32, (sends, peer), 0) % peer
             == lax.broadcasted_iota(jnp.int32, (sends, peer), 1))
    listed = jnp.sum(jnp.where(place, wide, 0.0), axis=1, keepdims=True)
    picks = (listed == lax.broadcasted_iota(jnp.int32, (sends, rows), 1).astype(F32)).astype(F32)
    own_rows = jnp.concatenate([src[0], src[1]], axis=0)
    rowsf[...] = mm(picks.astype(BF16), own_rows)
    for p in range(n_dom):
        outx[p] = rowsf[p * peer:(p + 1) * peer, :].astype(BF16)
    nr_ref[d] = outx[d]

    def nr_copy(r):
        p = (d + r) % n_dom
        return remote(outx.at[p], nr_ref.at[d], nr_s.at[r], nr_r.at[r], {"dom": p})

    relay(0)

    for c in range(n_cl):
        total = jnp.zeros((cl, depth), F32)
        for k in range(slots):
            tile = jnp.where(jnp.full((cl, cl), tcnt_ref[c], jnp.int32) > k, tile_ref[c, k], 0)
            total = total + mm(tile, src[tidx_ref[c, k]])
        hid[c * cl:(c + 1) * cl, :] = total.astype(BF16)
    turned = hid[...].astype(F32).T.astype(BF16)
    hid_t[...] = turned.reshape(n_pair, 2, blk, rows)
    for c in range(n_cl):
        for j in range(n_src):
            part = jnp.zeros((cl, cl), F32)
            for k in range(slots):
                live = (jnp.full((cl, cl), tcnt_ref[c], jnp.int32) > k) & (
                    jnp.full((cl, cl), tidx_ref[c, k], jnp.int32) == j)
                part = part + jnp.where(live, tile_ref[c, k].astype(F32), 0.0)
            part = part.T
            high = part.astype(BF16)
            op_hi[j, :, c * cl:(c + 1) * cl] = high
            op_lo[j, :, c * cl:(c + 1) * cl] = (part - high.astype(F32)).astype(BF16)

    def pt_copy(ch):
        return remote(ptx.at[ch], prx.at[ch], pt_s.at[ch], pt_r.at[ch], {"dom": partner})

    def st_copy(i, r):
        low = r
        return remote(stx.at[i, r], rrx.at[i, r], st_s.at[i, r], st_r.at[i, r],
                      {"dom": near(i, low) * 2 + core})

    def z_copy(r):
        to = (g + r) % n_group
        return remote(ztx.at[to // sub, to % sub], zrx.at[r], z_s.at[r], z_r.at[r], {"group": to})

    def f_copy(r):
        return remote(ftx, frx.at[r], f_s.at[r], f_r.at[r], {"group": (g + r) % n_group})

    def stage_a(i):
        ch = chunk(i)
        if i:
            relay(i)
        keep(i).wait()
        for r in range(n_pair):
            pa_copy(i, r).wait_recv()
        weight = wbuf[ch].reshape(depth, cw)
        if i == 0:
            loads[9].wait()
        preact = mm(hid[...], weight)
        s = jax.nn.sigmoid(preact)
        act_ref[:, cols(ch)] = (preact * s).astype(BF16)
        slope = s * (1.0 + preact * (1.0 - s))
        pg = (og_ref[:, cols(ch)].astype(F32) * slope).astype(BF16)
        pre[ch] = pg
        away = mm(hid_t[:, 1 - core].reshape(n_pair * blk, rows), pg)
        ptx[ch] = away.astype(BF16).reshape(n_pair, blk, cw)
        pt_copy(ch).start()
        here = mm(hid_t[:, core].reshape(n_pair * blk, rows), pg)
        own[ch] = here.reshape(n_pair, blk, cw)

    def stage_b(i):
        ch = chunk(i)
        pt_copy(ch).wait_recv()
        for r in [*range(1, n_pair), 0]:
            q = near(i, r)
            both = own[ch, q] + prx[ch, q].astype(F32)
            if r:
                stx[i, r] = both.astype(BF16)
                st_copy(i, r).start()
            else:
                work[i] = both

    def stage_c(i):
        ch = chunk(i)
        total = work[i]
        for r in range(1, n_pair):
            st_copy(i, r).wait_recv()
            total = total + rrx[i, r].astype(F32)
        acc[i] = total.reshape(sub, bs, cw)
        ztx[ch] = acc[i].astype(BF16)
        for h in range(sub):
            if i < nc - 1:
                z_copy((ch * sub + h - g + n_group) % n_group).start()
            elif h > 0:
                mate = ch * sub + (g + h) % sub
                z_copy((mate - g + n_group) % n_group).start()

    def step(n):
        if 0 <= n - 1 < nc:
            stage_b(n - 1)
        if 0 <= n - 2 < nc:
            stage_c(n - 2)

    for i in range(nc):
        stage_a(i)
        if i == 1:
            loads[10].wait()
        step(i)

    def back(m):
        part = jnp.zeros((rows, cw), F32)
        for c in range(nc):
            wpart = wbuf[c].reshape(depth, cw)[m * cw:(m + 1) * cw]
            part = part + lax.dot_general(pre[c], wpart, NT, preferred_element_type=F32)
        hgrad[:, m * cw:(m + 1) * cw] = part.astype(BF16)

    late = nc
    for m in range(nc):
        back(m)
        if m == nc // 2 - 1:
            step(late)

    def source_grad(j):
        return mm(op_hi[j], hgrad[...]) + mm(op_lo[j], hgrad[...])

    rowsf[...] = source_grad(n_src - 1)
    for p in range(n_dom):
        bgx[p] = rowsf[p * peer:(p + 1) * peer, :].astype(BF16)
    ng_ref[d] = bgx[d]

    def ng_copy(r):
        p = (d + r) % n_dom
        return remote(bgx.at[p], ng_ref.at[d], ng_s.at[r], ng_r.at[r], {"dom": p})

    for n in range(nc + 1, nc + 2):
        step(n)

    def swap(r):
        nr_copy(r).start()
        ng_copy(r).start()

    each(1, n_dom, swap)

    def gather(r):
        z_copy(r).wait_recv()
        acc[nc - 1, g % sub] = acc[nc - 1, g % sub] + zrx[r].astype(F32)

    each(1, n_group, gather)
    ftx[...] = acc[nc - 1, g % sub].astype(BF16)
    each(1, n_group, lambda r: f_copy(r).start())

    def store(owner, value):
        wg_ref[pl.ds(pl.multiple_of(owner % sub * bs, bs), bs), cols(owner // sub)] = value.astype(F32)

    store(g, ftx[...])

    for j in range(n_src - 1):
        back_rows = lax.dot_general(
            picks[:, j * cl:(j + 1) * cl].T.astype(BF16), sg_ref[...], (((1,), (0,)), ((), ())),
            preferred_element_type=F32)
        fg_ref[j * cl:(j + 1) * cl, :] = (source_grad(j) + back_rows).astype(BF16)

    def take(r):
        f_copy(r).wait_recv()
        store((g - r + n_group) % n_group, frx[r])

    each(1, n_group, take)

    def drain_dom(r):
        nr_copy(r).wait()
        ng_copy(r).wait()

    each(1, n_dom, drain_dom)
    for i in range(nc):
        ch = chunk(i)

        def drain(r):
            if i < nc - 1:
                ag_copy(i, r).wait_send()
            else:
                zw_copy(r).wait_send()
            pa_copy(i, r).wait_send()
            st_copy(i, r).wait_send()

        for r in range(1, n_pair):
            drain(r)
        pa_copy(i, 0).wait_send()
        pt_copy(ch).wait_send()

    def drain_group(r):
        z_copy(r).wait_send()
        f_copy(r).wait_send()

    each(1, n_group, drain_group)


def write_out(*refs):
    sems = refs[10]
    copies = [pltpu.make_async_copy(refs[n], refs[5 + n], sems.at[n]) for n in range(5)]
    for copy in copies:
        copy.start()
    for copy in copies:
        copy.wait()


def local(n_group, n_dom, hot_rows, cold_codes, scale_index, scale_table, stale_rows, tile_index,
          tile_count, tile_values, weight, out_grad, stale_grads, send_rows):
    blk, depth = weight.shape
    rows = out_grad.shape[0]
    cl = tile_values.shape[2]
    peer = send_rows.shape[1]
    n_pair = n_dom // 2
    nc, sub, bs, cw = pieces(n_group, blk, depth)
    n_src = rows // cl + stale_rows.shape[0] // cl
    vmem, hbm = pl.BlockSpec(memory_space=pltpu.VMEM), pl.BlockSpec(memory_space=pltpu.HBM)
    dma = pltpu.SemaphoreType.DMA
    out = pl.pallas_call(
        functools.partial(kernel, n_group, n_dom),
        out_shape=(
            jax.ShapeDtypeStruct((rows, depth), BF16),
            jax.ShapeDtypeStruct((rows, depth), BF16),
            jax.ShapeDtypeStruct((blk, depth), F32),
            jax.ShapeDtypeStruct((n_dom, peer, depth), BF16),
            jax.ShapeDtypeStruct((n_dom, peer, depth), BF16),
        ),
        in_specs=[hbm] * 12,
        out_specs=(vmem,) * 5,
        scratch_shapes=[
            pltpu.SMEM(tile_index.shape, jnp.int32),
            pltpu.SMEM(tile_count.shape, jnp.int32),
            pltpu.VMEM(cold_codes.shape, BF16),
            pltpu.VMEM((1, scale_index.shape[0]), jnp.int32),
            pltpu.VMEM((1, scale_table.shape[0]), F32),
            pltpu.VMEM(tile_values.shape, BF16),
            pltpu.VMEM(out_grad.shape, BF16),
            pltpu.VMEM(stale_grads.shape, BF16),
            pltpu.VMEM(send_rows.shape, jnp.int32),
            pltpu.VMEM((n_src, cl, depth), BF16),
            pltpu.VMEM((nc, n_dom, blk, cw), BF16),
            pltpu.VMEM((rows, depth), BF16),
            pltpu.VMEM((n_pair, 2, blk, rows), BF16),
            pltpu.VMEM((nc, rows, cw), BF16),
            pltpu.VMEM((nc, n_pair, blk, cw), BF16),
            pltpu.VMEM((nc, n_pair, blk, cw), BF16),
            pltpu.VMEM((nc, n_pair, blk, cw), F32),
            pltpu.VMEM((nc, blk, cw), F32),
            pltpu.VMEM((nc, n_pair, blk, cw), BF16),
            pltpu.VMEM((nc, n_pair, blk, cw), BF16),
            pltpu.VMEM((nc, sub, bs, cw), BF16),
            pltpu.VMEM((n_group, bs, cw), BF16),
            pltpu.VMEM((bs, cw), BF16),
            pltpu.VMEM((n_group, bs, cw), BF16),
            pltpu.VMEM((nc, sub, bs, cw), F32),
            pltpu.VMEM((n_dom * peer, depth), F32),
            pltpu.VMEM((n_dom, peer, depth), BF16),
            pltpu.VMEM((n_dom, peer, depth), BF16),
            pltpu.VMEM((n_src, cl, rows), BF16),
            pltpu.VMEM((n_src, cl, rows), BF16),
            pltpu.VMEM((rows, depth), BF16),
            dma((11,)), dma((nc,)),
            dma((nc, n_pair)), dma((nc, n_pair)), dma((n_pair,)), dma((n_pair,)), dma((nc, n_pair)), dma((nc, n_pair)),
            dma((n_dom,)), dma((n_dom,)), dma((n_dom,)), dma((n_dom,)),
            dma((nc,)), dma((nc,)), dma((nc, n_pair)), dma((nc, n_pair)),
            dma((n_group,)), dma((n_group,)), dma((n_group,)), dma((n_group,)),
        ],
        compiler_params=pltpu.CompilerParams(
            collective_id=0, has_side_effects=True, vmem_limit_bytes=48 * 1024 * 1024),
    )(*[pltpu.with_memory_space_constraint(a, pltpu.HBM) for a in (
        tile_index, tile_count, hot_rows, cold_codes, scale_index.reshape(1, -1),
        scale_table.reshape(1, -1), stale_rows, tile_values, weight, out_grad, stale_grads,
        send_rows)])
    act, fg, wg, nr, ng = pl.pallas_call(
        write_out,
        out_shape=tuple(jax.ShapeDtypeStruct(o.shape, o.dtype) for o in out),
        in_specs=[vmem] * 5,
        out_specs=(hbm,) * 5,
        scratch_shapes=[dma((5,))],
        compiler_params=pltpu.CompilerParams(vmem_limit_bytes=8 * 1024 * 1024),
    )(*out)
    return act, fg, wg, nr.reshape(-1, depth), ng.reshape(-1, depth)


def solution(mesh):
    both = ("group", "dom")
    return jax.shard_map(
        functools.partial(local, mesh.shape["group"], mesh.shape["dom"]),
        mesh=mesh,
        in_specs=(
            P(both, None), P(both, None), P(both), P(), P(both, None), P(both, None), P(both),
            P(both, None, None, None), P("dom", None), P(both, None), P(both, None), P(both, None),
        ),
        out_specs=(P(both, None), P(both, None), P("dom", None), P(both, None), P(both, None)),
        check_vma=False,
    )
```
